768 devices in a mesh: gz: 32 (over x, z_lo, core), ch: 24 (over z_hi, y).
Axes of the slice: x: 4, y: 8, z: 12 (z_hi: 3, z_lo: 4; z = z_hi * 4 + z_lo), core: 2. Of those that a mesh axis runs over, the one named last changes fastest.
Arguments:
- inputs: bfloat16 [64, 192, 6144], P('gz', 'ch'), may hold values from -6 to 6
- out_grad: bfloat16 [64, 192, 6144], P('gz', 'ch'), may hold values from -6 to 6
- filters: bfloat16 [864, 32], replicated, may hold values from -0.21875 to 0.21875
Outputs:
- in_grad: bfloat16 [64, 192, 6144], P('gz', 'ch')
- filter_grad: float32 [864, 32], replicated
The draws below stay inside these ranges and needn't reach their ends.
All inputs are finite; a program needn't handle non-finite values.
Results may differ from the reference program's by a relative error of at most 0.001.
Values may be sent and summed in bfloat16 or wider, within the bound.
A program may use at most 32 MiB of HBM per device.

```python
import jax
import jax.numpy as jnp
from jax import lax

CH = 32
NX = 192
NZ = 64
NY = 192
CELLS = 2359296


def shard_levels(key, dims, pieces, low, largest):
    def one(dim, parts):
        draws = jax.random.uniform(jax.random.fold_in(jax.random.fold_in(key, 6), dim), (parts,), jnp.float32, low / len(pieces), largest / len(pieces))
        return jnp.repeat(jnp.exp(draws), dims[dim] // parts).reshape((-1,) + (1,) * (len(dims) - dim - 1))

    level = one(*pieces[0])
    for cut in pieces[1:]:
        level = level * one(*cut)
    return level


def gaussian(own_key, shape, width, reach, pieces=(), kind=jnp.bfloat16):
    result = width * jax.random.normal(own_key, shape, jnp.float32)
    if pieces:
        result = result * shard_levels(own_key, shape, pieces, -0.22, 0.18)
    return jnp.clip(result, -reach, reach).astype(kind)


def setup_inputs(seed: int = 0) -> dict:
    keys = jax.random.split(jax.random.key(seed), 4)
    inputs = gaussian(keys[0], (NZ, NY, NX * CH), 1.0, 6.0, ((0, 32), (1, 24)))
    out_grad = gaussian(keys[1], (NZ, NY, NX * CH), 1.0, 6.0, ((0, 32), (1, 24)))
    filters = gaussian(keys[2], (27 * CH, CH), (27 * CH) ** -0.5, 0.21875)
    return {"inputs": inputs, "out_grad": out_grad, "filters": filters}


def forward(values, kernel):
    padded = jnp.pad(values, ((0, 0), (1, 1), (1, 1), (1, 1), (0, 0)), mode='wrap')
    return lax.conv_general_dilated(padded, kernel, (1, 1, 1), 'VALID', dimension_numbers=('NDHWC', 'DHWIO', 'NDHWC'), precision=lax.Precision.HIGHEST)

def reference(inputs, out_grad, filters):
    values = inputs.astype(jnp.float32).reshape(1, NZ, NY, NX, CH)
    kernel = filters.astype(jnp.float32).reshape(3, 3, 3, CH, CH)
    upstream = out_grad.astype(jnp.float32).reshape(1, NZ, NY, NX, CH)
    outputs, pullback = jax.vjp(forward, values, kernel)
    grad_values, grad_kernel = pullback(upstream)
    in_grad = grad_values.reshape(NZ, NY, NX * CH).astype(jnp.bfloat16)
    scale = jnp.float32(1.0) / jnp.sqrt(jnp.float32(CELLS))
    filter_grad = grad_kernel.reshape(27 * CH, CH).astype(jnp.float32) * scale
    return (in_grad, filter_grad)
```

```python
import functools

import jax
import jax.numpy as jnp
from jax import lax
from jax.experimental import pallas as pl
from jax.experimental.pallas import tpu as pltpu
from jax.sharding import PartitionSpec as P

MESH = pl.DeviceIdType.MESH
CH = 32
LANES = 128
PACK = LANES // CH
PIECES = 64
TAPS = 27


def kernel(
    geometry,
    scale,
    x_hbm,
    og_hbm,
    f_hbm,
    in_grad,
    filter_grad,
    x_v,
    og_v,
    f_v,
    rows32,
    edge,
    z_low,
    z_high,
    y_side,
    y_side32,
    tail,
    bands,
    xt,
    windows,
    grads,
    pieces,
    parts,
    layers,
    whole,
    local_sem,
    halo_send,
    halo_recv,
    ring_send,
    ring_recv,
):
    n_x, n_zlo, n_core, n_zhi, n_y = geometry
    depth, height, width = x_hbm.shape
    groups = width // LANES
    group_rows = depth * height
    n_gz, n_ch = n_x * n_zlo * n_core, n_zhi * n_y
    n_plane, n_z = n_x * n_y * n_core, n_zhi * n_zlo

    gz, ch = lax.axis_index("gz"), lax.axis_index("ch")
    core = lax.rem(gz, n_core)
    z_lo = lax.rem(gz // n_core, n_zlo)
    x = gz // (n_core * n_zlo)
    z_hi, y = ch // n_y, lax.rem(ch, n_y)
    rank = (x * n_y + y) * n_core + core
    z = z_hi * n_zlo + z_lo

    def plane_device(r):
        r_core, r_y, r_x = lax.rem(r, n_core), lax.rem(r // n_core, n_y), r // (n_core * n_y)
        return ((r_x * n_zlo + z_lo) * n_core + r_core, z_hi * n_y + r_y)

    def z_device(r):
        return ((x * n_zlo + lax.rem(r, n_zlo)) * n_core + core, (r // n_zlo) * n_y + y)

    up, down = lax.rem(gz + 1, n_gz), lax.rem(gz + n_gz - 1, n_gz)
    right, left = lax.rem(ch + 1, n_ch), lax.rem(ch + n_ch - 1, n_ch)
    neighbours = [(up, ch), (down, ch), (gz, right), (gz, left), (up, right), (down, right), (up, left), (down, left)]

    loads = [
        pltpu.make_async_copy(og_hbm, og_v, local_sem.at[0]),
        pltpu.make_async_copy(x_hbm, x_v, local_sem.at[1]),
        pltpu.make_async_copy(f_hbm, f_v, local_sem.at[2]),
    ]
    for load in loads:
        load.start()

    barrier = pltpu.get_barrier_semaphore()
    for device in neighbours:
        pl.semaphore_signal(barrier, inc=1, device_id=device, device_id_type=MESH)

    @pl.loop(1, n_z)
    def _(d):
        pl.semaphore_signal(barrier, inc=1, device_id=z_device(lax.rem(z + d, n_z)), device_id_type=MESH)

    @pl.loop(1, n_plane)
    def _(d):
        pl.semaphore_signal(
            barrier, inc=1, device_id=plane_device(lax.rem(rank + d, n_plane)), device_id_type=MESH
        )

    lane = lax.broadcasted_iota(jnp.int32, (height, LANES), 1) // CH
    row = lax.broadcasted_iota(jnp.int32, (height, LANES), 0)

    def tile(ref, layer, g):
        return ref[layer, :, g * LANES : (g + 1) * LANES].astype(jnp.float32)

    loads[0].wait()
    for layer in range(depth):
        for g in range(groups):
            block = tile(og_v, layer, g)
            rows32[layer, g : g + 1, :] = block[0:1]
            rows32[depth + layer, g : g + 1, :] = block[height - 1 : height]
    for k in range(2 * depth):
        edge[k] = rows32[k].astype(jnp.bfloat16)

    loads[2].wait()
    wide = lax.broadcasted_iota(jnp.int32, (CH, LANES), 1) // CH
    last = f_v.shape[1] // LANES
    tiles = [f_v[:, k * LANES : (k + 1) * LANES].astype(jnp.float32) for k in range(last)]
    tail[:, : f_v.shape[1] - last * LANES] = f_v[:, last * LANES :].astype(jnp.float32)
    tiles.append(tail[...])
    for w in range(9):
        place, turn = (3 * w) // PACK, (3 * w) % PACK
        slab = tiles[place]
        if turn:
            joined = slab if turn == 1 else jnp.where(wide >= turn, slab, tiles[place + 1])
            slab = pltpu.roll(joined, LANES - CH * turn, 1)
        for c_from in range(PACK):
            start = w * LANES + c_from * CH
            turn = (c_from - 1) % PACK
            band = pltpu.roll(slab, CH * turn, 1) if turn else slab
            used = wide != (c_from + 2) % PACK
            inside = used
            outside = jnp.zeros_like(band)
            if c_from == 0:
                inside = wide < 2
                outside = jnp.where(wide == PACK - 1, band, 0.0)
            elif c_from == PACK - 1:
                inside = wide >= 2
                outside = jnp.where(wide == 0, band, 0.0)
            bands[start : start + CH, :LANES] = jnp.where(inside, band, 0.0).astype(jnp.bfloat16)
            bands[start : start + CH, LANES:] = outside.astype(jnp.bfloat16)

    loads[1].wait()
    blocks = [jnp.concatenate([tile(x_v, layer, g) for layer in range(depth)], axis=0) for g in range(groups)]
    tall = lax.broadcasted_iota(jnp.int32, (group_rows, LANES), 1) // CH
    step = 8
    for g0 in range(0, groups, step):
        own = jnp.concatenate(blocks[g0 : g0 + step], axis=0)
        outer = jnp.concatenate(
            [
                jnp.where(tall < PACK // 2, blocks[(g + 1) % groups], blocks[(g - 1) % groups])
                for g in range(g0, g0 + step)
            ],
            axis=0,
        )
        columns = slice(g0 * group_rows, (g0 + step) * group_rows)
        xt[0:LANES, columns] = own.T.astype(jnp.bfloat16)
        xt[LANES : 2 * LANES, columns] = outer.T.astype(jnp.bfloat16)

    pl.semaphore_wait(barrier, len(neighbours) + (n_z - 1) + (n_plane - 1))

    halo = [
        (edge.at[pl.ds(depth, depth)], y_side.at[0, pl.ds(1, depth)]),
        (edge.at[pl.ds(0, depth)], y_side.at[1, pl.ds(1, depth)]),
        (edge.at[depth + depth - 1], y_side.at[0, 0]),
        (edge.at[depth], y_side.at[0, depth + 1]),
        (edge.at[depth - 1], y_side.at[1, 0]),
        (edge.at[0], y_side.at[1, depth + 1]),
    ]
    halo = [(og_v.at[depth - 1], z_low), (og_v.at[0], z_high)] + halo
    sends = [
        pltpu.make_async_remote_copy(
            src_ref=source,
            dst_ref=target,
            send_sem=halo_send.at[k],
            recv_sem=halo_recv.at[k],
            device_id=neighbours[k],
            device_id_type=MESH,
        )
        for k, (source, target) in enumerate(halo)
    ]
    for k in (4, 5, 6, 7, 2, 3, 0, 1):
        sends[k].start()
    for send in sends:
        send.wait_recv()

    for side in range(2):
        for layer in range(depth + 2):
            y_side32[side, layer] = y_side[side, layer].astype(jnp.float32)

    for g in range(groups):
        cut = slice(g * LANES, (g + 1) * LANES)
        planes = [z_low[:, cut].astype(jnp.float32)]
        planes += [tile(og_v, layer, g) for layer in range(depth)]
        planes += [z_high[:, cut].astype(jnp.float32)]
        moved = [[], planes, []]
        for layer, plane in enumerate(planes):
            low = jnp.broadcast_to(y_side32[0, layer, g : g + 1, :], plane.shape)
            high = jnp.broadcast_to(y_side32[1, layer, g : g + 1, :], plane.shape)
            moved[2].append(jnp.where(row == 0, low, pltpu.roll(plane, 1, 0)))
            moved[0].append(jnp.where(row == height - 1, high, pltpu.roll(plane, height - 1, 0)))
        for kz in range(3):
            for ky in range(3):
                w = 3 * kz + ky
                block = jnp.concatenate(moved[ky][2 - kz : 2 - kz + depth], axis=0)
                windows[g * group_rows : (g + 1) * group_rows, w * LANES : (w + 1) * LANES] = block.astype(
                    jnp.bfloat16
                )

    grads[...] = jnp.dot(xt[...], windows[...], preferred_element_type=jnp.float32)

    def blocks_of(tap, t):
        if tap >= TAPS:
            return jnp.zeros((8, LANES), jnp.float32)
        w, kx = tap // 3, tap % 3
        total = None
        for c_from in range(PACK):
            c = c_from + kx - 1
            block = c if 0 <= c < PACK else (PACK if c == PACK else 2 * PACK - 1)
            start = block * CH + t * 8
            value = grads[start : start + 8, w * LANES : (w + 1) * LANES]
            total = value if total is None else jnp.where(lane == c_from, value, total)
        return total

    near, even = lane < 2, lane % 2 == 0
    for half in range(2):
        for k in range(PACK):
            for t in range(PACK):
                sums = [blocks_of(PACK * (PACK * half + n) + k, t) for n in range(PACK)]
                first = jnp.where(near, sums[0], sums[2]) + pltpu.roll(jnp.where(near, sums[2], sums[0]), 64, 1)
                second = jnp.where(near, sums[1], sums[3]) + pltpu.roll(jnp.where(near, sums[3], sums[1]), 64, 1)
                other = jnp.where(even, second, first)
                packed = jnp.where(even, first, second) + jnp.where(
                    even, pltpu.roll(other, LANES - CH, 1), pltpu.roll(other, CH, 1)
                )
                place = 2 * ((half * PACK + k) * PACK + t)
                pieces[place] = packed[0:4]
                pieces[place + 1] = packed[4:8]

    def plane_copy(d, source, target):
        return pltpu.make_async_remote_copy(
            src_ref=source,
            dst_ref=target,
            send_sem=ring_send.at[0],
            recv_sem=ring_recv.at[0],
            device_id=plane_device(lax.rem(rank + d, n_plane)),
            device_id_type=MESH,
        )

    @pl.loop(1, n_plane)
    def _(d):
        plane_copy(d, pieces.at[lax.rem(rank + d, n_plane)], parts.at[n_plane - 1 - d]).start()

    wide_out = lax.dot_general(
        windows[...], bands[...], (((1,), (0,)), ((), ())), preferred_element_type=jnp.float32
    )
    own = wide_out[:, :LANES]
    outer = wide_out[:, LANES:]
    for g in range(groups):
        for layer in range(depth):

            def rows(value, group, layer=layer):
                start = (group % groups) * group_rows + layer * height
                return value[start : start + height]

            result = rows(own, g) + jnp.where(lane < PACK // 2, rows(outer, g - 1), rows(outer, g + 1))
            in_grad[layer, :, g * LANES : (g + 1) * LANES] = result.astype(jnp.bfloat16)

    def all_but_one(ref, sem):
        count = ref.shape[0] - 1
        return pltpu.make_async_copy(ref.at[pl.ds(0, count)], ref.at[pl.ds(0, count)], ring_recv.at[sem])

    pltpu.make_async_copy(parts, parts, ring_recv.at[0]).wait()
    total = pieces[rank]
    for k in range(n_plane - 1):
        total = total + parts[k]
    layers[z] = total

    @pl.loop(1, n_z)
    def _(d):
        pltpu.make_async_remote_copy(
            src_ref=layers.at[z],
            dst_ref=layers.at[z],
            send_sem=ring_send.at[1],
            recv_sem=ring_recv.at[1],
            device_id=z_device(lax.rem(z + d, n_z)),
            device_id_type=MESH,
        ).start()

    all_but_one(layers, 1).wait()
    total = layers[0]
    for k in range(1, n_z):
        total = total + layers[k]
    whole[rank] = total * scale

    @pl.loop(1, n_plane)
    def _(d):
        pltpu.make_async_remote_copy(
            src_ref=whole.at[rank],
            dst_ref=whole.at[rank],
            send_sem=ring_send.at[2],
            recv_sem=ring_recv.at[2],
            device_id=plane_device(lax.rem(rank + d, n_plane)),
            device_id_type=MESH,
        ).start()

    all_but_one(whole, 2).wait()
    for half in range(2):
        start = half * PIECES // 2
        block = jnp.concatenate([whole[start + k] for k in range(PIECES // 2)], axis=0).T
        for n in range(PACK):
            column = (half * PACK + n) * LANES
            count = min(LANES, f_v.shape[1] - column)
            if count > 0:
                filter_grad[:, column : column + count] = block[n * CH : (n + 1) * CH, :count]

    for send in sends:
        send.wait_send()
    pltpu.make_async_copy(parts, parts, ring_send.at[0]).wait()
    pltpu.make_async_copy(layers.at[pl.ds(0, n_z - 1)], layers.at[pl.ds(0, n_z - 1)], ring_send.at[1]).wait()
    pltpu.make_async_copy(parts, parts, ring_send.at[2]).wait()


def per_device(geometry, inputs, out_grad, filters):
    depth, height, width = inputs.shape
    filters = filters.T
    n_x, n_zlo, n_core, n_zhi, n_y = geometry
    n_plane, n_z = n_x * n_y * n_core, n_zhi * n_zlo
    groups = width // LANES
    rows = depth * height * groups
    bf16, f32 = jnp.bfloat16, jnp.float32
    scratch = [
        pltpu.VMEM((depth, height, width), bf16),
        pltpu.VMEM((depth, height, width), bf16),
        pltpu.VMEM(filters.shape, bf16),
        pltpu.VMEM((2 * depth, groups, LANES), f32),
        pltpu.VMEM((2 * depth, groups, LANES), bf16),
        pltpu.VMEM((height, width), bf16),
        pltpu.VMEM((height, width), bf16),
        pltpu.VMEM((2, depth + 2, groups, LANES), bf16),
        pltpu.VMEM((2, depth + 2, groups, LANES), f32),
        pltpu.VMEM((CH, LANES), f32),
        pltpu.VMEM((9 * LANES, 2 * LANES), bf16),
        pltpu.VMEM((2 * LANES, rows), bf16),
        pltpu.VMEM((rows, 9 * LANES), bf16),
        pltpu.VMEM((2 * LANES, 9 * LANES), f32),
        pltpu.VMEM((PIECES, 4, LANES), f32),
        pltpu.VMEM((n_plane - 1, 4, LANES), f32),
        pltpu.VMEM((n_z, 4, LANES), f32),
        pltpu.VMEM((n_plane, 4, LANES), f32),
        pltpu.SemaphoreType.DMA((3,)),
        pltpu.SemaphoreType.DMA((8,)),
        pltpu.SemaphoreType.DMA((8,)),
        pltpu.SemaphoreType.DMA((3,)),
        pltpu.SemaphoreType.DMA((3,)),
    ]
    cells = rows * PACK * n_plane * n_z
    scale = float(1.0 / (cells**0.5))
    in_grad, filter_grad = pl.pallas_call(
        functools.partial(kernel, geometry, scale),
        out_shape=(
            jax.ShapeDtypeStruct(inputs.shape, bf16),
            jax.ShapeDtypeStruct(filters.shape, f32),
        ),
        in_specs=[pl.BlockSpec(memory_space=pltpu.HBM)] * 3,
        out_specs=[pl.BlockSpec(memory_space=pltpu.VMEM)] * 2,
        scratch_shapes=scratch,
        compiler_params=pltpu.CompilerParams(
            collective_id=0, has_side_effects=True, vmem_limit_bytes=48 * 1024 * 1024
        ),
    )(inputs, out_grad, filters)
    return in_grad, filter_grad.T


def solution(mesh):
    n_gz, n_ch = mesh.shape["gz"], mesh.shape["ch"]
    n_zlo, n_core, n_zhi = 4, 2, 3
    geometry = (n_gz // (n_zlo * n_core), n_zlo, n_core, n_zhi, n_ch // n_zhi)
    placed = (P("gz", "ch", None), P("gz", "ch", None), P())
    return jax.shard_map(
        functools.partial(per_device, geometry),
        mesh=mesh,
        in_specs=placed,
        out_specs=(P("gz", "ch", None), P()),
        check_vma=False,
    )
```

```python
import functools

import jax
import jax.numpy as jnp
from jax import lax
from jax.experimental import pallas as pl
from jax.experimental.pallas import tpu as pltpu
from jax.sharding import PartitionSpec as P

MESH = pl.DeviceIdType.MESH
CH = 32
LANES = 128
PACK = LANES // CH
PIECES = 64
TAPS = 27


def kernel(
    geometry,
    scale,
    x_hbm,
    og_hbm,
    f_hbm,
    in_grad,
    filter_grad,
    x_v,
    og_v,
    f_v,
    rows32,
    edge,
    z_low,
    z_high,
    y_side,
    y_side32,
    tail,
    bands,
    xt,
    windows,
    grads,
    pieces,
    parts,
    layers,
    whole,
    local_sem,
    halo_send,
    halo_recv,
    ring_send,
    ring_recv,
):
    n_x, n_zlo, n_core, n_zhi, n_y = geometry
    depth, height, width = x_hbm.shape
    groups = width // LANES
    group_rows = depth * height
    n_gz, n_ch = n_x * n_zlo * n_core, n_zhi * n_y
    n_plane, n_z = n_x * n_y * n_core, n_zhi * n_zlo

    gz, ch = lax.axis_index("gz"), lax.axis_index("ch")
    core = lax.rem(gz, n_core)
    z_lo = lax.rem(gz // n_core, n_zlo)
    x = gz // (n_core * n_zlo)
    z_hi, y = ch // n_y, lax.rem(ch, n_y)
    rank = (x * n_y + y) * n_core + core
    z = z_hi * n_zlo + z_lo

    def ways(size):
        return sorted(range(size), key=lambda move: -min(move, size - move))

    def moved(place, move, size):
        return place if move == 0 else lax.rem(place + move, size)

    x_at = [moved(x, move, n_x) for move in range(n_x)]
    core_at = [moved(core, move, n_core) for move in range(n_core)]
    near_moves = [(mx, mc) for mx in ways(n_x) for mc in ways(n_core)]

    def plane_walk(act):
        def row(my, there, alone):
            for mx, mc in near_moves:
                if alone and mx == 0 and mc == 0:
                    continue
                gz_there = (x_at[mx] * n_zlo + z_lo) * n_core + core_at[mc]
                rank_there = (x_at[mx] * n_y + there) * n_core + core_at[mc]
                act((gz_there, z_hi * n_y + there), rank_there, my * (n_x * n_core) + mx * n_core + mc - 1)

        half = n_y // 2
        row(half, lax.rem(y + half, n_y), False)

        @pl.loop(1, half)
        def _(j):
            row(half + j, lax.rem(y + half + j, n_y), False)
            row(half - j, lax.rem(y + half - j, n_y), False)

        row(0, y, True)

    z_moves = [(mh, ml) for mh in ways(n_zhi) for ml in ways(n_zlo) if mh or ml]
    z_peers = [
        ((x * n_zlo + moved(z_lo, ml, n_zlo)) * n_core + core, moved(z_hi, mh, n_zhi) * n_y + y) for mh, ml in z_moves
    ]

    up, down = lax.rem(gz + 1, n_gz), lax.rem(gz + n_gz - 1, n_gz)
    right, left = lax.rem(ch + 1, n_ch), lax.rem(ch + n_ch - 1, n_ch)
    neighbours = [(up, ch), (down, ch), (gz, right), (gz, left), (up, right), (down, right), (up, left), (down, left)]

    loads = [
        pltpu.make_async_copy(og_hbm, og_v, local_sem.at[0]),
        pltpu.make_async_copy(x_hbm, x_v, local_sem.at[1]),
        pltpu.make_async_copy(f_hbm, f_v, local_sem.at[2]),
    ]
    for load in loads:
        load.start()

    barrier = pltpu.get_barrier_semaphore()
    for device in neighbours:
        pl.semaphore_signal(barrier, inc=1, device_id=device, device_id_type=MESH)

    def greet(device, *_):
        pl.semaphore_signal(barrier, inc=1, device_id=device, device_id_type=MESH)

    plane_walk(greet)
    for device in z_peers:
        greet(device)

    lane = lax.broadcasted_iota(jnp.int32, (height, LANES), 1) // CH
    row = lax.broadcasted_iota(jnp.int32, (height, LANES), 0)

    def tile(ref, layer, g):
        return ref[layer, :, g * LANES : (g + 1) * LANES].astype(jnp.float32)

    loads[0].wait()
    for layer in range(depth):
        for g in range(groups):
            block = tile(og_v, layer, g)
            rows32[layer, g : g + 1, :] = block[0:1]
            rows32[depth + layer, g : g + 1, :] = block[height - 1 : height]
    for k in range(2 * depth):
        edge[k] = rows32[k].astype(jnp.bfloat16)

    pl.semaphore_wait(barrier, len(neighbours) + (n_z - 1) + (n_plane - 1))

    halo = [
        (edge.at[pl.ds(depth, depth)], y_side.at[0, pl.ds(1, depth)]),
        (edge.at[pl.ds(0, depth)], y_side.at[1, pl.ds(1, depth)]),
        (edge.at[depth + depth - 1], y_side.at[0, 0]),
        (edge.at[depth], y_side.at[0, depth + 1]),
        (edge.at[depth - 1], y_side.at[1, 0]),
        (edge.at[0], y_side.at[1, depth + 1]),
    ]
    halo = [(og_v.at[depth - 1], z_low), (og_v.at[0], z_high)] + halo
    sends = [
        pltpu.make_async_remote_copy(
            src_ref=source,
            dst_ref=target,
            send_sem=halo_send.at[k],
            recv_sem=halo_recv.at[k],
            device_id=neighbours[k],
            device_id_type=MESH,
        )
        for k, (source, target) in enumerate(halo)
    ]
    for k in (4, 5, 6, 7, 2, 3, 0, 1):
        sends[k].start()
    loads[2].wait()
    wide = lax.broadcasted_iota(jnp.int32, (CH, LANES), 1) // CH
    last = f_v.shape[1] // LANES
    tiles = [f_v[:, k * LANES : (k + 1) * LANES].astype(jnp.float32) for k in range(last)]
    tail[:, : f_v.shape[1] - last * LANES] = f_v[:, last * LANES :].astype(jnp.float32)
    tiles.append(tail[...])
    for w in range(9):
        place, turn = (3 * w) // PACK, (3 * w) % PACK
        slab = tiles[place]
        if turn:
            joined = slab if turn == 1 else jnp.where(wide >= turn, slab, tiles[place + 1])
            slab = pltpu.roll(joined, LANES - CH * turn, 1)
        for c_from in range(PACK):
            start = w * LANES + c_from * CH
            turn = (c_from - 1) % PACK
            band = pltpu.roll(slab, CH * turn, 1) if turn else slab
            used = wide != (c_from + 2) % PACK
            inside = used
            outside = jnp.zeros_like(band)
            if c_from == 0:
                inside = wide < 2
                outside = jnp.where(wide == PACK - 1, band, 0.0)
            elif c_from == PACK - 1:
                inside = wide >= 2
                outside = jnp.where(wide == 0, band, 0.0)
            bands[start : start + CH, :LANES] = jnp.where(inside, band, 0.0).astype(jnp.bfloat16)
            bands[start : start + CH, LANES:] = outside.astype(jnp.bfloat16)

    loads[1].wait()
    blocks = [jnp.concatenate([tile(x_v, layer, g) for layer in range(depth)], axis=0) for g in range(groups)]
    tall = lax.broadcasted_iota(jnp.int32, (group_rows, LANES), 1) // CH
    step = 8
    for g0 in range(0, groups, step):
        own = jnp.concatenate(blocks[g0 : g0 + step], axis=0)
        outer = jnp.concatenate(
            [
                jnp.where(tall < PACK // 2, blocks[(g + 1) % groups], blocks[(g - 1) % groups])
                for g in range(g0, g0 + step)
            ],
            axis=0,
        )
        columns = slice(g0 * group_rows, (g0 + step) * group_rows)
        xt[0:LANES, columns] = own.T.astype(jnp.bfloat16)
        xt[LANES : 2 * LANES, columns] = outer.T.astype(jnp.bfloat16)

    for send in sends:
        send.wait_recv()

    for side in range(2):
        for layer in range(depth + 2):
            y_side32[side, layer] = y_side[side, layer].astype(jnp.float32)

    for g in range(groups):
        cut = slice(g * LANES, (g + 1) * LANES)
        planes = [z_low[:, cut].astype(jnp.float32)]
        planes += [tile(og_v, layer, g) for layer in range(depth)]
        planes += [z_high[:, cut].astype(jnp.float32)]
        turned = [[], planes, []]
        for layer, plane in enumerate(planes):
            low = jnp.broadcast_to(y_side32[0, layer, g : g + 1, :], plane.shape)
            high = jnp.broadcast_to(y_side32[1, layer, g : g + 1, :], plane.shape)
            turned[2].append(jnp.where(row == 0, low, pltpu.roll(plane, 1, 0)))
            turned[0].append(jnp.where(row == height - 1, high, pltpu.roll(plane, height - 1, 0)))
        for kz in range(3):
            for ky in range(3):
                w = 3 * kz + ky
                block = jnp.concatenate(turned[ky][2 - kz : 2 - kz + depth], axis=0)
                windows[g * group_rows : (g + 1) * group_rows, w * LANES : (w + 1) * LANES] = block.astype(
                    jnp.bfloat16
                )

    grads[...] = jnp.dot(xt[...], windows[...], preferred_element_type=jnp.float32)

    def blocks_of(tap, t):
        if tap >= TAPS:
            return jnp.zeros((8, LANES), jnp.float32)
        w, kx = tap // 3, tap % 3
        total = None
        for c_from in range(PACK):
            c = c_from + kx - 1
            block = c if 0 <= c < PACK else (PACK if c == PACK else 2 * PACK - 1)
            start = block * CH + t * 8
            value = grads[start : start + 8, w * LANES : (w + 1) * LANES]
            total = value if total is None else jnp.where(lane == c_from, value, total)
        return total

    near, even = lane < 2, lane % 2 == 0
    for half in range(2):
        for k in range(PACK):
            for t in range(PACK):
                sums = [blocks_of(PACK * (PACK * half + n) + k, t) for n in range(PACK)]
                first = jnp.where(near, sums[0], sums[2]) + pltpu.roll(jnp.where(near, sums[2], sums[0]), 64, 1)
                second = jnp.where(near, sums[1], sums[3]) + pltpu.roll(jnp.where(near, sums[3], sums[1]), 64, 1)
                other = jnp.where(even, second, first)
                packed = jnp.where(even, first, second) + jnp.where(
                    even, pltpu.roll(other, LANES - CH, 1), pltpu.roll(other, CH, 1)
                )
                place = 2 * ((half * PACK + k) * PACK + t)
                pieces[place] = packed[0:4]
                pieces[place + 1] = packed[4:8]

    def send_part(device, rank_there, offset):
        pltpu.make_async_remote_copy(
            src_ref=pieces.at[rank_there],
            dst_ref=parts.at[offset],
            send_sem=ring_send.at[0],
            recv_sem=ring_recv.at[0],
            device_id=device,
            device_id_type=MESH,
        ).start()

    plane_walk(send_part)

    wide_out = lax.dot_general(
        windows[...], bands[...], (((1,), (0,)), ((), ())), preferred_element_type=jnp.float32
    )
    own = wide_out[:, :LANES]
    outer = wide_out[:, LANES:]
    for g in range(groups):
        for layer in range(depth):

            def rows(value, group, layer=layer):
                start = (group % groups) * group_rows + layer * height
                return value[start : start + height]

            result = rows(own, g) + jnp.where(lane < PACK // 2, rows(outer, g - 1), rows(outer, g + 1))
            in_grad[layer, :, g * LANES : (g + 1) * LANES] = result.astype(jnp.bfloat16)

    def all_but_one(ref, sem):
        count = ref.shape[0] - 1
        return pltpu.make_async_copy(ref.at[pl.ds(0, count)], ref.at[pl.ds(0, count)], ring_recv.at[sem])

    pltpu.make_async_copy(parts, parts, ring_recv.at[0]).wait()
    total = pieces[rank]
    for k in range(n_plane - 1):
        total = total + parts[k]
    layers[z] = total

    for device in z_peers:
        pltpu.make_async_remote_copy(
            src_ref=layers.at[z],
            dst_ref=layers.at[z],
            send_sem=ring_send.at[1],
            recv_sem=ring_recv.at[1],
            device_id=device,
            device_id_type=MESH,
        ).start()

    all_but_one(layers, 1).wait()
    total = layers[0]
    for k in range(1, n_z):
        total = total + layers[k]
    whole[rank] = total * scale

    def send_whole(device, *_):
        pltpu.make_async_remote_copy(
            src_ref=whole.at[rank],
            dst_ref=whole.at[rank],
            send_sem=ring_send.at[2],
            recv_sem=ring_recv.at[2],
            device_id=device,
            device_id_type=MESH,
        ).start()

    plane_walk(send_whole)

    all_but_one(whole, 2).wait()
    for half in range(2):
        start = half * PIECES // 2
        block = jnp.concatenate([whole[start + k] for k in range(PIECES // 2)], axis=0).T
        for n in range(PACK):
            column = (half * PACK + n) * LANES
            count = min(LANES, f_v.shape[1] - column)
            if count > 0:
                filter_grad[:, column : column + count] = block[n * CH : (n + 1) * CH, :count]

    for send in sends:
        send.wait_send()
    pltpu.make_async_copy(parts, parts, ring_send.at[0]).wait()
    pltpu.make_async_copy(layers.at[pl.ds(0, n_z - 1)], layers.at[pl.ds(0, n_z - 1)], ring_send.at[1]).wait()
    pltpu.make_async_copy(parts, parts, ring_send.at[2]).wait()


def per_device(geometry, inputs, out_grad, filters):
    depth, height, width = inputs.shape
    filters = filters.T
    n_x, n_zlo, n_core, n_zhi, n_y = geometry
    n_plane, n_z = n_x * n_y * n_core, n_zhi * n_zlo
    groups = width // LANES
    rows = depth * height * groups
    bf16, f32 = jnp.bfloat16, jnp.float32
    scratch = [
        pltpu.VMEM((depth, height, width), bf16),
        pltpu.VMEM((depth, height, width), bf16),
        pltpu.VMEM(filters.shape, bf16),
        pltpu.VMEM((2 * depth, groups, LANES), f32),
        pltpu.VMEM((2 * depth, groups, LANES), bf16),
        pltpu.VMEM((height, width), bf16),
        pltpu.VMEM((height, width), bf16),
        pltpu.VMEM((2, depth + 2, groups, LANES), bf16),
        pltpu.VMEM((2, depth + 2, groups, LANES), f32),
        pltpu.VMEM((CH, LANES), f32),
        pltpu.VMEM((9 * LANES, 2 * LANES), bf16),
        pltpu.VMEM((2 * LANES, rows), bf16),
        pltpu.VMEM((rows, 9 * LANES), bf16),
        pltpu.VMEM((2 * LANES, 9 * LANES), f32),
        pltpu.VMEM((PIECES, 4, LANES), f32),
        pltpu.VMEM((n_plane - 1, 4, LANES), f32),
        pltpu.VMEM((n_z, 4, LANES), f32),
        pltpu.VMEM((n_plane, 4, LANES), f32),
        pltpu.SemaphoreType.DMA((3,)),
        pltpu.SemaphoreType.DMA((8,)),
        pltpu.SemaphoreType.DMA((8,)),
        pltpu.SemaphoreType.DMA((3,)),
        pltpu.SemaphoreType.DMA((3,)),
    ]
    cells = rows * PACK * n_plane * n_z
    scale = float(1.0 / (cells**0.5))
    in_grad, filter_grad = pl.pallas_call(
        functools.partial(kernel, geometry, scale),
        out_shape=(
            jax.ShapeDtypeStruct(inputs.shape, bf16),
            jax.ShapeDtypeStruct(filters.shape, f32),
        ),
        in_specs=[pl.BlockSpec(memory_space=pltpu.HBM)] * 3,
        out_specs=[pl.BlockSpec(memory_space=pltpu.VMEM)] * 2,
        scratch_shapes=scratch,
        compiler_params=pltpu.CompilerParams(
            collective_id=0, has_side_effects=True, vmem_limit_bytes=48 * 1024 * 1024
        ),
    )(*(pltpu.with_memory_space_constraint(value, pltpu.HBM) for value in (inputs, out_grad, filters)))
    return in_grad, filter_grad.T


def solution(mesh):
    n_gz, n_ch = mesh.shape["gz"], mesh.shape["ch"]
    n_zlo, n_core, n_zhi = 4, 2, 3
    geometry = (n_gz // (n_zlo * n_core), n_zlo, n_core, n_zhi, n_ch // n_zhi)
    placed = (P("gz", "ch", None), P("gz", "ch", None), P())
    return jax.shard_map(
        functools.partial(per_device, geometry),
        mesh=mesh,
        in_specs=placed,
        out_specs=(P("gz", "ch", None), P()),
        check_vma=False,
    )
```

```python
import functools

import jax
import jax.numpy as jnp
from jax import lax
from jax.experimental import pallas as pl
from jax.experimental.pallas import tpu as pltpu
from jax.sharding import PartitionSpec as P

MESH = pl.DeviceIdType.MESH
CH = 32
LANES = 128
PACK = LANES // CH
PIECES = 64
TAPS = 27


def kernel(
    geometry,
    scale,
    x_hbm,
    og_hbm,
    f_hbm,
    in_grad,
    filter_grad,
    x_v,
    og_v,
    f_v,
    rows32,
    edge,
    z_low,
    z_high,
    y_side,
    y_side32,
    tail,
    bands,
    xt,
    windows,
    grads,
    pieces,
    parts,
    layers,
    whole,
    local_sem,
    halo_send,
    halo_recv,
    ring_send,
    ring_recv,
):
    n_x, n_zlo, n_core, n_zhi, n_y = geometry
    depth, height, width = x_hbm.shape
    groups = width // LANES
    group_rows = depth * height
    n_gz, n_ch = n_x * n_zlo * n_core, n_zhi * n_y
    n_plane, n_z = n_x * n_y * n_core, n_zhi * n_zlo

    gz, ch = lax.axis_index("gz"), lax.axis_index("ch")
    core = lax.rem(gz, n_core)
    z_lo = lax.rem(gz // n_core, n_zlo)
    x = gz // (n_core * n_zlo)
    z_hi, y = ch // n_y, lax.rem(ch, n_y)
    rank = (x * n_y + y) * n_core + core
    z = z_hi * n_zlo + z_lo

    def ways(size):
        return sorted(range(size), key=lambda move: -min(move, size - move))

    def moved(place, move, size):
        return place if move == 0 else lax.rem(place + move, size)

    x_at = [moved(x, move, n_x) for move in range(n_x)]
    core_at = [moved(core, move, n_core) for move in range(n_core)]
    near_moves = [(mx, mc) for mx in ways(n_x) for mc in ways(n_core)]

    def plane_walk(act):
        def row(my, there, alone):
            for mx, mc in near_moves:
                if alone and mx == 0 and mc == 0:
                    continue
                gz_there = (x_at[mx] * n_zlo + z_lo) * n_core + core_at[mc]
                rank_there = (x_at[mx] * n_y + there) * n_core + core_at[mc]
                act((gz_there, z_hi * n_y + there), rank_there, my * (n_x * n_core) + mx * n_core + mc - 1)

        half = n_y // 2
        row(half, lax.rem(y + half, n_y), False)

        @pl.loop(1, half)
        def _(j):
            row(half + j, lax.rem(y + half + j, n_y), False)
            row(half - j, lax.rem(y + half - j, n_y), False)

        row(0, y, True)

    z_moves = [(mh, ml) for mh in ways(n_zhi) for ml in ways(n_zlo) if mh or ml]
    z_peers = [
        ((x * n_zlo + moved(z_lo, ml, n_zlo)) * n_core + core, moved(z_hi, mh, n_zhi) * n_y + y) for mh, ml in z_moves
    ]

    up, down = lax.rem(gz + 1, n_gz), lax.rem(gz + n_gz - 1, n_gz)
    right, left = lax.rem(ch + 1, n_ch), lax.rem(ch + n_ch - 1, n_ch)
    neighbours = [(up, ch), (down, ch), (gz, right), (gz, left), (up, right), (down, right), (up, left), (down, left)]

    loads = [
        pltpu.make_async_copy(og_hbm, og_v, local_sem.at[0]),
        pltpu.make_async_copy(x_hbm, x_v, local_sem.at[1]),
        pltpu.make_async_copy(f_hbm, f_v, local_sem.at[2]),
    ]
    for load in loads:
        load.start()

    barrier = pltpu.get_barrier_semaphore()
    for device in neighbours:
        pl.semaphore_signal(barrier, inc=1, device_id=device, device_id_type=MESH)

    def greet(device, *_):
        pl.semaphore_signal(barrier, inc=1, device_id=device, device_id_type=MESH)

    plane_walk(greet)
    for device in z_peers:
        greet(device)

    lane = lax.broadcasted_iota(jnp.int32, (height, LANES), 1) // CH
    row = lax.broadcasted_iota(jnp.int32, (height, LANES), 0)

    def tile(ref, layer, g):
        return ref[layer, :, g * LANES : (g + 1) * LANES].astype(jnp.float32)

    loads[0].wait()
    for layer in range(depth):
        for g in range(groups):
            block = tile(og_v, layer, g)
            rows32[layer, g : g + 1, :] = block[0:1]
            rows32[depth + layer, g : g + 1, :] = block[height - 1 : height]
    for k in range(2 * depth):
        edge[k] = rows32[k].astype(jnp.bfloat16)

    pl.semaphore_wait(barrier, len(neighbours) + (n_z - 1) + (n_plane - 1))

    halo = [
        (edge.at[pl.ds(depth, depth)], y_side.at[0, pl.ds(1, depth)]),
        (edge.at[pl.ds(0, depth)], y_side.at[1, pl.ds(1, depth)]),
        (edge.at[depth + depth - 1], y_side.at[0, 0]),
        (edge.at[depth], y_side.at[0, depth + 1]),
        (edge.at[depth - 1], y_side.at[1, 0]),
        (edge.at[0], y_side.at[1, depth + 1]),
    ]
    halo = [(og_v.at[depth - 1], z_low), (og_v.at[0], z_high)] + halo
    sends = [
        pltpu.make_async_remote_copy(
            src_ref=source,
            dst_ref=target,
            send_sem=halo_send.at[k],
            recv_sem=halo_recv.at[k],
            device_id=neighbours[k],
            device_id_type=MESH,
        )
        for k, (source, target) in enumerate(halo)
    ]
    for k in (4, 5, 6, 7, 2, 3, 0, 1):
        sends[k].start()
    loads[2].wait()
    wide = lax.broadcasted_iota(jnp.int32, (CH, LANES), 1) // CH
    last = f_v.shape[1] // LANES
    tiles = [f_v[:, k * LANES : (k + 1) * LANES].astype(jnp.float32) for k in range(last)]
    tail[:, : f_v.shape[1] - last * LANES] = f_v[:, last * LANES :].astype(jnp.float32)
    tiles.append(tail[...])
    for w in range(9):
        place, turn = (3 * w) // PACK, (3 * w) % PACK
        slab = tiles[place]
        if turn:
            joined = slab if turn == 1 else jnp.where(wide >= turn, slab, tiles[place + 1])
            slab = pltpu.roll(joined, LANES - CH * turn, 1)
        for c_from in range(PACK):
            start = w * LANES + c_from * CH
            turn = (c_from - 1) % PACK
            band = pltpu.roll(slab, CH * turn, 1) if turn else slab
            used = wide != (c_from + 2) % PACK
            inside = used
            outside = jnp.zeros_like(band)
            if c_from == 0:
                inside = wide < 2
                outside = jnp.where(wide == PACK - 1, band, 0.0)
            elif c_from == PACK - 1:
                inside = wide >= 2
                outside = jnp.where(wide == 0, band, 0.0)
            bands[start : start + CH, :LANES] = jnp.where(inside, band, 0.0).astype(jnp.bfloat16)
            bands[start : start + CH, LANES:] = outside.astype(jnp.bfloat16)

    loads[1].wait()
    blocks = [jnp.concatenate([tile(x_v, layer, g) for layer in range(depth)], axis=0) for g in range(groups)]
    tall = lax.broadcasted_iota(jnp.int32, (group_rows, LANES), 1) // CH
    step = 8
    for g0 in range(0, groups, step):
        own = jnp.concatenate(blocks[g0 : g0 + step], axis=0)
        outer = jnp.concatenate(
            [
                jnp.where(tall < PACK // 2, blocks[(g + 1) % groups], blocks[(g - 1) % groups])
                for g in range(g0, g0 + step)
            ],
            axis=0,
        )
        columns = slice(g0 * group_rows, (g0 + step) * group_rows)
        xt[0:LANES, columns] = own.T.astype(jnp.bfloat16)
        xt[LANES : 2 * LANES, columns] = outer.T.astype(jnp.bfloat16)

    for send in sends:
        send.wait_recv()

    for side in range(2):
        for layer in range(depth + 2):
            y_side32[side, layer] = y_side[side, layer].astype(jnp.float32)

    for g in range(groups):
        cut = slice(g * LANES, (g + 1) * LANES)
        planes = [z_low[:, cut].astype(jnp.float32)]
        planes += [tile(og_v, layer, g) for layer in range(depth)]
        planes += [z_high[:, cut].astype(jnp.float32)]
        turned = [[], planes, []]
        for layer, plane in enumerate(planes):
            low = jnp.broadcast_to(y_side32[0, layer, g : g + 1, :], plane.shape)
            high = jnp.broadcast_to(y_side32[1, layer, g : g + 1, :], plane.shape)
            turned[2].append(jnp.where(row == 0, low, pltpu.roll(plane, 1, 0)))
            turned[0].append(jnp.where(row == height - 1, high, pltpu.roll(plane, height - 1, 0)))
        for kz in range(3):
            for ky in range(3):
                w = 3 * kz + ky
                block = jnp.concatenate(turned[ky][2 - kz : 2 - kz + depth], axis=0)
                windows[g * group_rows : (g + 1) * group_rows, w * LANES : (w + 1) * LANES] = block.astype(
                    jnp.bfloat16
                )

    grads[...] = jnp.dot(xt[...], windows[...], preferred_element_type=jnp.float32)

    def blocks_of(tap, t):
        if tap >= TAPS:
            return jnp.zeros((8, LANES), jnp.float32)
        w, kx = tap // 3, tap % 3
        total = None
        for c_from in range(PACK):
            c = c_from + kx - 1
            block = c if 0 <= c < PACK else (PACK if c == PACK else 2 * PACK - 1)
            start = block * CH + t * 8
            value = grads[start : start + 8, w * LANES : (w + 1) * LANES]
            total = value if total is None else jnp.where(lane == c_from, value, total)
        return total

    near, even = lane < 2, lane % 2 == 0
    for half in range(2):
        for k in range(PACK):
            for t in range(PACK):
                sums = [blocks_of(PACK * (PACK * half + n) + k, t) for n in range(PACK)]
                first = jnp.where(near, sums[0], sums[2]) + pltpu.roll(jnp.where(near, sums[2], sums[0]), 64, 1)
                second = jnp.where(near, sums[1], sums[3]) + pltpu.roll(jnp.where(near, sums[3], sums[1]), 64, 1)
                other = jnp.where(even, second, first)
                packed = jnp.where(even, first, second) + jnp.where(
                    even, pltpu.roll(other, LANES - CH, 1), pltpu.roll(other, CH, 1)
                )
                place = 2 * ((half * PACK + k) * PACK + t)
                pieces[place] = packed[0:4]
                pieces[place + 1] = packed[4:8]

    def send_part(device, rank_there, offset):
        pltpu.make_async_remote_copy(
            src_ref=pieces.at[rank_there],
            dst_ref=parts.at[offset],
            send_sem=ring_send.at[0],
            recv_sem=ring_recv.at[0],
            device_id=device,
            device_id_type=MESH,
        ).start()

    plane_walk(send_part)

    wide_out = lax.dot_general(
        windows[...], bands[...], (((1,), (0,)), ((), ())), preferred_element_type=jnp.float32
    )
    own = wide_out[:, :LANES]
    outer = wide_out[:, LANES:]
    for g in range(groups):
        for layer in range(depth):

            def rows(value, group, layer=layer):
                start = (group % groups) * group_rows + layer * height
                return value[start : start + height]

            result = rows(own, g) + jnp.where(lane < PACK // 2, rows(outer, g - 1), rows(outer, g + 1))
            in_grad[layer, :, g * LANES : (g + 1) * LANES] = result.astype(jnp.bfloat16)

    def all_but_one(ref, sem):
        count = ref.shape[0] - 1
        return pltpu.make_async_copy(ref.at[pl.ds(0, count)], ref.at[pl.ds(0, count)], ring_recv.at[sem])

    pltpu.make_async_copy(parts, parts, ring_recv.at[0]).wait()
    total = pieces[rank]
    for k in range(n_plane - 1):
        total = total + parts[k]
    layers[z] = total

    for device in z_peers:
        pltpu.make_async_remote_copy(
            src_ref=layers.at[z],
            dst_ref=layers.at[z],
            send_sem=ring_send.at[1],
            recv_sem=ring_recv.at[1],
            device_id=device,
            device_id_type=MESH,
        ).start()

    all_but_one(layers, 1).wait()
    total = layers[0]
    for k in range(1, n_z):
        total = total + layers[k]
    whole[rank] = total * scale

    def send_whole(device, *_):
        pltpu.make_async_remote_copy(
            src_ref=whole.at[rank],
            dst_ref=whole.at[rank],
            send_sem=ring_send.at[2],
            recv_sem=ring_recv.at[2],
            device_id=device,
            device_id_type=MESH,
        ).start()

    plane_walk(send_whole)

    all_but_one(whole, 2).wait()
    for half in range(2):
        start = half * PIECES // 2
        block = jnp.concatenate([whole[start + k] for k in range(PIECES // 2)], axis=0).T
        for n in range(PACK):
            column = (half * PACK + n) * LANES
            count = min(LANES, f_v.shape[1] - column)
            if count > 0:
                filter_grad[:, column : column + count] = block[n * CH : (n + 1) * CH, :count]

    for send in sends:
        send.wait_send()
    pltpu.make_async_copy(parts, parts, ring_send.at[0]).wait()
    pltpu.make_async_copy(layers.at[pl.ds(0, n_z - 1)], layers.at[pl.ds(0, n_z - 1)], ring_send.at[1]).wait()
    pltpu.make_async_copy(parts, parts, ring_send.at[2]).wait()


def put_out(in_grad_v, filter_grad_v, in_grad, filter_grad, sems):
    copies = [
        pltpu.make_async_copy(filter_grad_v, filter_grad, sems.at[0]),
        pltpu.make_async_copy(in_grad_v, in_grad, sems.at[1]),
    ]
    for copy in copies:
        copy.start()
    for copy in copies:
        copy.wait()


def per_device(geometry, inputs, out_grad, filters):
    depth, height, width = inputs.shape
    filters = filters.T
    n_x, n_zlo, n_core, n_zhi, n_y = geometry
    n_plane, n_z = n_x * n_y * n_core, n_zhi * n_zlo
    groups = width // LANES
    rows = depth * height * groups
    bf16, f32 = jnp.bfloat16, jnp.float32
    scratch = [
        pltpu.VMEM((depth, height, width), bf16),
        pltpu.VMEM((depth, height, width), bf16),
        pltpu.VMEM(filters.shape, bf16),
        pltpu.VMEM((2 * depth, groups, LANES), f32),
        pltpu.VMEM((2 * depth, groups, LANES), bf16),
        pltpu.VMEM((height, width), bf16),
        pltpu.VMEM((height, width), bf16),
        pltpu.VMEM((2, depth + 2, groups, LANES), bf16),
        pltpu.VMEM((2, depth + 2, groups, LANES), f32),
        pltpu.VMEM((CH, LANES), f32),
        pltpu.VMEM((9 * LANES, 2 * LANES), bf16),
        pltpu.VMEM((2 * LANES, rows), bf16),
        pltpu.VMEM((rows, 9 * LANES), bf16),
        pltpu.VMEM((2 * LANES, 9 * LANES), f32),
        pltpu.VMEM((PIECES, 4, LANES), f32),
        pltpu.VMEM((n_plane - 1, 4, LANES), f32),
        pltpu.VMEM((n_z, 4, LANES), f32),
        pltpu.VMEM((n_plane, 4, LANES), f32),
        pltpu.SemaphoreType.DMA((3,)),
        pltpu.SemaphoreType.DMA((8,)),
        pltpu.SemaphoreType.DMA((8,)),
        pltpu.SemaphoreType.DMA((3,)),
        pltpu.SemaphoreType.DMA((3,)),
    ]
    cells = rows * PACK * n_plane * n_z
    scale = float(1.0 / (cells**0.5))
    in_grad, filter_grad = pl.pallas_call(
        functools.partial(kernel, geometry, scale),
        out_shape=(
            jax.ShapeDtypeStruct(inputs.shape, bf16),
            jax.ShapeDtypeStruct(filters.shape, f32),
        ),
        in_specs=[pl.BlockSpec(memory_space=pltpu.HBM)] * 3,
        out_specs=[pl.BlockSpec(memory_space=pltpu.VMEM)] * 2,
        scratch_shapes=scratch,
        compiler_params=pltpu.CompilerParams(
            collective_id=0, has_side_effects=True, vmem_limit_bytes=48 * 1024 * 1024
        ),
    )(*(pltpu.with_memory_space_constraint(value, pltpu.HBM) for value in (inputs, out_grad, filters)))
    in_grad, filter_grad = pl.pallas_call(
        put_out,
        out_shape=(
            jax.ShapeDtypeStruct(in_grad.shape, bf16),
            jax.ShapeDtypeStruct(filter_grad.shape, f32),
        ),
        in_specs=[pl.BlockSpec(memory_space=pltpu.VMEM)] * 2,
        out_specs=[pl.BlockSpec(memory_space=pltpu.HBM)] * 2,
        scratch_shapes=[pltpu.SemaphoreType.DMA((2,))],
        compiler_params=pltpu.CompilerParams(vmem_limit_bytes=8 * 1024 * 1024),
    )(in_grad, filter_grad)
    return in_grad, filter_grad.T


def solution(mesh):
    n_gz, n_ch = mesh.shape["gz"], mesh.shape["ch"]
    n_zlo, n_core, n_zhi = 4, 2, 3
    geometry = (n_gz // (n_zlo * n_core), n_zlo, n_core, n_zhi, n_ch // n_zhi)
    placed = (P("gz", "ch", None), P("gz", "ch", None), P())
    return jax.shard_map(
        functools.partial(per_device, geometry),
        mesh=mesh,
        in_specs=placed,
        out_specs=(P("gz", "ch", None), P()),
        check_vma=False,
    )
```

```python
import functools

import jax
import jax.numpy as jnp
from jax import lax
from jax.experimental import pallas as pl
from jax.experimental.pallas import tpu as pltpu
from jax.sharding import PartitionSpec as P

MESH = pl.DeviceIdType.MESH
CH = 32
LANES = 128
PACK = LANES // CH
PIECES = 32
TAPS = 27


def kernel(
    geometry,
    scale,
    x_hbm,
    og_hbm,
    f_hbm,
    in_grad,
    filter_grad,
    x_v,
    og_v,
    f_v,
    rows32,
    edge,
    z_low,
    z_high,
    y_side,
    y_side32,
    tail,
    bands,
    xt,
    windows,
    grads,
    pieces,
    parts,
    layers,
    whole,
    local_sem,
    halo_send,
    halo_recv,
    ring_send,
    ring_recv,
):
    n_x, n_zlo, n_core, n_zhi, n_y = geometry
    depth, height, width = x_hbm.shape
    groups = width // LANES
    group_rows = depth * height
    n_gz, n_ch = n_x * n_zlo * n_core, n_zhi * n_y
    n_plane, n_z = n_x * n_y * n_core, n_zhi * n_zlo

    gz, ch = lax.axis_index("gz"), lax.axis_index("ch")
    core = lax.rem(gz, n_core)
    z_lo = lax.rem(gz // n_core, n_zlo)
    x = gz // (n_core * n_zlo)
    z_hi, y = ch // n_y, lax.rem(ch, n_y)
    rank = (x * n_y + y) * n_core + core
    z = z_hi * n_zlo + z_lo

    def ways(size):
        return sorted(range(size), key=lambda move: -min(move, size - move))

    def moved(place, move, size):
        return place if move == 0 else lax.rem(place + move, size)

    x_at = [moved(x, move, n_x) for move in range(n_x)]
    core_at = [moved(core, move, n_core) for move in range(n_core)]
    near_moves = [(mx, mc) for mx in ways(n_x) for mc in ways(n_core)]

    def plane_walk(act):
        def row(my, there, alone):
            for mx, mc in near_moves:
                if alone and mx == 0 and mc == 0:
                    continue
                gz_there = (x_at[mx] * n_zlo + z_lo) * n_core + core_at[mc]
                rank_there = (x_at[mx] * n_y + there) * n_core + core_at[mc]
                act((gz_there, z_hi * n_y + there), rank_there, my * (n_x * n_core) + mx * n_core + mc - 1)

        half = n_y // 2
        row(half, lax.rem(y + half, n_y), False)

        @pl.loop(1, half)
        def _(j):
            row(half + j, lax.rem(y + half + j, n_y), False)
            row(half - j, lax.rem(y + half - j, n_y), False)

        row(0, y, True)

    owner_rows = [(n_y - 2 + k) % n_y for k in range(4)]
    own_row = lax.rem(y + 2, n_y)
    owner = own_row < len(owner_rows)
    mine = (x * len(owner_rows) + lax.rem(own_row, len(owner_rows))) * n_core + core

    z_moves = [(mh, ml) for mh in ways(n_zhi) for ml in ways(n_zlo) if mh or ml]
    z_peers = [
        ((x * n_zlo + moved(z_lo, ml, n_zlo)) * n_core + core, moved(z_hi, mh, n_zhi) * n_y + y) for mh, ml in z_moves
    ]

    up, down = lax.rem(gz + 1, n_gz), lax.rem(gz + n_gz - 1, n_gz)
    right, left = lax.rem(ch + 1, n_ch), lax.rem(ch + n_ch - 1, n_ch)
    neighbours = [(up, ch), (down, ch), (gz, right), (gz, left), (up, right), (down, right), (up, left), (down, left)]

    loads = [
        pltpu.make_async_copy(og_hbm, og_v, local_sem.at[0]),
        pltpu.make_async_copy(x_hbm, x_v, local_sem.at[1]),
        pltpu.make_async_copy(f_hbm, f_v, local_sem.at[2]),
    ]
    for load in loads:
        load.start()

    barrier = pltpu.get_barrier_semaphore()
    for device in neighbours:
        pl.semaphore_signal(barrier, inc=1, device_id=device, device_id_type=MESH)

    def greet(device, *_):
        pl.semaphore_signal(barrier, inc=1, device_id=device, device_id_type=MESH)

    plane_walk(greet)
    for device in z_peers:
        greet(device)

    lane = lax.broadcasted_iota(jnp.int32, (height, LANES), 1) // CH
    row = lax.broadcasted_iota(jnp.int32, (height, LANES), 0)

    def tile(ref, layer, g):
        return ref[layer, :, g * LANES : (g + 1) * LANES].astype(jnp.float32)

    loads[0].wait()
    for layer in range(depth):
        for g in range(groups):
            block = tile(og_v, layer, g)
            rows32[layer, g : g + 1, :] = block[0:1]
            rows32[depth + layer, g : g + 1, :] = block[height - 1 : height]
    for k in range(2 * depth):
        edge[k] = rows32[k].astype(jnp.bfloat16)

    pl.semaphore_wait(barrier, len(neighbours) + (n_z - 1) + (n_plane - 1))

    halo = [
        (edge.at[pl.ds(depth, depth)], y_side.at[0, pl.ds(1, depth)]),
        (edge.at[pl.ds(0, depth)], y_side.at[1, pl.ds(1, depth)]),
        (edge.at[depth + depth - 1], y_side.at[0, 0]),
        (edge.at[depth], y_side.at[0, depth + 1]),
        (edge.at[depth - 1], y_side.at[1, 0]),
        (edge.at[0], y_side.at[1, depth + 1]),
    ]
    halo = [(og_v.at[depth - 1], z_low), (og_v.at[0], z_high)] + halo
    sends = [
        pltpu.make_async_remote_copy(
            src_ref=source,
            dst_ref=target,
            send_sem=halo_send.at[k],
            recv_sem=halo_recv.at[k],
            device_id=neighbours[k],
            device_id_type=MESH,
        )
        for k, (source, target) in enumerate(halo)
    ]
    for k in (4, 5, 6, 7, 2, 3, 0, 1):
        sends[k].start()
    loads[2].wait()
    wide = lax.broadcasted_iota(jnp.int32, (CH, LANES), 1) // CH
    last = f_v.shape[1] // LANES
    tiles = [f_v[:, k * LANES : (k + 1) * LANES].astype(jnp.float32) for k in range(last)]
    tail[:, : f_v.shape[1] - last * LANES] = f_v[:, last * LANES :].astype(jnp.float32)
    tiles.append(tail[...])
    for w in range(9):
        place, turn = (3 * w) // PACK, (3 * w) % PACK
        slab = tiles[place]
        if turn:
            joined = slab if turn == 1 else jnp.where(wide >= turn, slab, tiles[place + 1])
            slab = pltpu.roll(joined, LANES - CH * turn, 1)
        for c_from in range(PACK):
            start = w * LANES + c_from * CH
            turn = (c_from - 1) % PACK
            band = pltpu.roll(slab, CH * turn, 1) if turn else slab
            used = wide != (c_from + 2) % PACK
            inside = used
            outside = jnp.zeros_like(band)
            if c_from == 0:
                inside = wide < 2
                outside = jnp.where(wide == PACK - 1, band, 0.0)
            elif c_from == PACK - 1:
                inside = wide >= 2
                outside = jnp.where(wide == 0, band, 0.0)
            bands[start : start + CH, :LANES] = jnp.where(inside, band, 0.0).astype(jnp.bfloat16)
            bands[start : start + CH, LANES:] = outside.astype(jnp.bfloat16)

    loads[1].wait()
    blocks = [jnp.concatenate([tile(x_v, layer, g) for layer in range(depth)], axis=0) for g in range(groups)]
    tall = lax.broadcasted_iota(jnp.int32, (group_rows, LANES), 1) // CH
    step = 8
    for g0 in range(0, groups, step):
        own = jnp.concatenate(blocks[g0 : g0 + step], axis=0)
        outer = jnp.concatenate(
            [
                jnp.where(tall < PACK // 2, blocks[(g + 1) % groups], blocks[(g - 1) % groups])
                for g in range(g0, g0 + step)
            ],
            axis=0,
        )
        columns = slice(g0 * group_rows, (g0 + step) * group_rows)
        xt[0:LANES, columns] = own.T.astype(jnp.bfloat16)
        xt[LANES : 2 * LANES, columns] = outer.T.astype(jnp.bfloat16)

    def planes_of(g):
        cut = slice(g * LANES, (g + 1) * LANES)
        planes = [z_low[:, cut].astype(jnp.float32)]
        planes += [tile(og_v, layer, g) for layer in range(depth)]
        return planes + [z_high[:, cut].astype(jnp.float32)]

    def put_window(g, ky, planes):
        for kz in range(3):
            w = 3 * kz + ky
            block = jnp.concatenate(planes[2 - kz : 2 - kz + depth], axis=0)
            windows[g * group_rows : (g + 1) * group_rows, w * LANES : (w + 1) * LANES] = block.astype(jnp.bfloat16)

    for send in sends[:2]:
        send.wait_recv()
    for g in range(groups):
        put_window(g, 1, planes_of(g))
    for send in sends[2:]:
        send.wait_recv()

    for side in range(2):
        for layer in range(depth + 2):
            y_side32[side, layer] = y_side[side, layer].astype(jnp.float32)

    for g in range(groups):
        before, after = [], []
        for layer, plane in enumerate(planes_of(g)):
            low = jnp.broadcast_to(y_side32[0, layer, g : g + 1, :], plane.shape)
            high = jnp.broadcast_to(y_side32[1, layer, g : g + 1, :], plane.shape)
            before.append(jnp.where(row == height - 1, high, pltpu.roll(plane, height - 1, 0)))
            after.append(jnp.where(row == 0, low, pltpu.roll(plane, 1, 0)))
        put_window(g, 0, before)
        put_window(g, 2, after)

    grads[...] = jnp.dot(xt[...], windows[...], preferred_element_type=jnp.float32)

    def blocks_of(tap, t):
        if tap >= TAPS:
            return jnp.zeros((8, LANES), jnp.float32)
        w, kx = tap // 3, tap % 3
        total = None
        for c_from in range(PACK):
            c = c_from + kx - 1
            block = c if 0 <= c < PACK else (PACK if c == PACK else 2 * PACK - 1)
            start = block * CH + t * 8
            value = grads[start : start + 8, w * LANES : (w + 1) * LANES]
            total = value if total is None else jnp.where(lane == c_from, value, total)
        return total

    near, even = lane < 2, lane % 2 == 0
    for half in range(2):
        for k in range(PACK):
            for t in range(PACK):
                sums = [blocks_of(PACK * (PACK * half + n) + k, t) for n in range(PACK)]
                first = jnp.where(near, sums[0], sums[2]) + pltpu.roll(jnp.where(near, sums[2], sums[0]), 64, 1)
                second = jnp.where(near, sums[1], sums[3]) + pltpu.roll(jnp.where(near, sums[3], sums[1]), 64, 1)
                other = jnp.where(even, second, first)
                packed = jnp.where(even, first, second) + jnp.where(
                    even, pltpu.roll(other, LANES - CH, 1), pltpu.roll(other, CH, 1)
                )
                pieces[(half * PACK + k) * PACK + t] = packed

    for mx, mc in near_moves:
        for k, there in enumerate(owner_rows):

            def send_part(mx=mx, mc=mc, k=k, there=there):
                pltpu.make_async_remote_copy(
                    src_ref=pieces.at[(x_at[mx] * len(owner_rows) + k) * n_core + core_at[mc]],
                    dst_ref=parts.at[y * (n_x * n_core) + mx * n_core + mc],
                    send_sem=ring_send.at[0],
                    recv_sem=ring_recv.at[0],
                    device_id=((x_at[mx] * n_zlo + z_lo) * n_core + core_at[mc], z_hi * n_y + there),
                    device_id_type=MESH,
                ).start()

            if mx == 0 and mc == 0:
                pl.when(y != there)(send_part)
            else:
                send_part()

    wide_out = lax.dot_general(
        windows[...], bands[...], (((1,), (0,)), ((), ())), preferred_element_type=jnp.float32
    )
    own = wide_out[:, :LANES]
    outer = wide_out[:, LANES:]
    for g in range(groups):
        for layer in range(depth):

            def rows(value, group, layer=layer):
                start = (group % groups) * group_rows + layer * height
                return value[start : start + height]

            result = rows(own, g) + jnp.where(lane < PACK // 2, rows(outer, g - 1), rows(outer, g + 1))
            in_grad[layer, :, g * LANES : (g + 1) * LANES] = result.astype(jnp.bfloat16)

    def all_but_one(ref, sem):
        count = ref.shape[0] - 1
        return pltpu.make_async_copy(ref.at[pl.ds(0, count)], ref.at[pl.ds(0, count)], ring_recv.at[sem])

    def spent(ref, count, sem):
        return pltpu.make_async_copy(ref.at[pl.ds(0, count)], ref.at[pl.ds(0, count)], sem)

    @pl.when(owner)
    def _():
        parts[y * (n_x * n_core)] = pieces[mine]
        all_but_one(parts, 0).wait()
        total = parts[0]
        for k in range(1, n_plane):
            total = total + parts[k]
        layers[z] = total
        for device in z_peers:
            pltpu.make_async_remote_copy(
                src_ref=layers.at[z],
                dst_ref=layers.at[z],
                send_sem=ring_send.at[1],
                recv_sem=ring_recv.at[1],
                device_id=device,
                device_id_type=MESH,
            ).start()
        all_but_one(layers, 1).wait()
        total = layers[0]
        for k in range(1, n_z):
            total = total + layers[k]
        whole[mine] = total * scale

        for there in sorted(range(n_y), key=lambda line: min(line, n_y - line)):
            for mx, mc in near_moves:

                def send_whole(mx=mx, mc=mc, there=there):
                    pltpu.make_async_remote_copy(
                        src_ref=whole.at[mine],
                        dst_ref=whole.at[mine],
                        send_sem=ring_send.at[2],
                        recv_sem=ring_recv.at[2],
                        device_id=((x_at[mx] * n_zlo + z_lo) * n_core + core_at[mc], z_hi * n_y + there),
                        device_id_type=MESH,
                    ).start()

                if mx == 0 and mc == 0:
                    pl.when(y != there)(send_whole)
                else:
                    send_whole()

        all_but_one(whole, 2).wait()

    @pl.when(jnp.logical_not(owner))
    def _():
        spent(whole, PIECES, ring_recv.at[2]).wait()

    for half in range(2):
        start = half * PIECES // 2
        block = jnp.concatenate([whole[start + k] for k in range(PIECES // 2)], axis=0).T
        for n in range(PACK):
            column = (half * PACK + n) * LANES
            count = min(LANES, f_v.shape[1] - column)
            if count > 0:
                filter_grad[:, column : column + count] = block[n * CH : (n + 1) * CH, :count]

    for send in sends:
        send.wait_send()
    @pl.when(owner)
    def _():
        spent(pieces, PIECES - 1, ring_send.at[0]).wait()
        spent(layers, n_z - 1, ring_send.at[1]).wait()
        spent(parts, n_plane - 1, ring_send.at[2]).wait()

    @pl.when(jnp.logical_not(owner))
    def _():
        spent(pieces, PIECES, ring_send.at[0]).wait()


def put_out(in_grad_v, filter_grad_v, in_grad, filter_grad, sems):
    copies = [
        pltpu.make_async_copy(filter_grad_v, filter_grad, sems.at[0]),
        pltpu.make_async_copy(in_grad_v, in_grad, sems.at[1]),
    ]
    for copy in copies:
        copy.start()
    for copy in copies:
        copy.wait()


def per_device(geometry, inputs, out_grad, filters):
    depth, height, width = inputs.shape
    filters = filters.T
    n_x, n_zlo, n_core, n_zhi, n_y = geometry
    n_plane, n_z = n_x * n_y * n_core, n_zhi * n_zlo
    groups = width // LANES
    rows = depth * height * groups
    bf16, f32 = jnp.bfloat16, jnp.float32
    scratch = [
        pltpu.VMEM((depth, height, width), bf16),
        pltpu.VMEM((depth, height, width), bf16),
        pltpu.VMEM(filters.shape, bf16),
        pltpu.VMEM((2 * depth, groups, LANES), f32),
        pltpu.VMEM((2 * depth, groups, LANES), bf16),
        pltpu.VMEM((height, width), bf16),
        pltpu.VMEM((height, width), bf16),
        pltpu.VMEM((2, depth + 2, groups, LANES), bf16),
        pltpu.VMEM((2, depth + 2, groups, LANES), f32),
        pltpu.VMEM((CH, LANES), f32),
        pltpu.VMEM((9 * LANES, 2 * LANES), bf16),
        pltpu.VMEM((2 * LANES, rows), bf16),
        pltpu.VMEM((rows, 9 * LANES), bf16),
        pltpu.VMEM((2 * LANES, 9 * LANES), f32),
        pltpu.VMEM((PIECES, 8, LANES), f32),
        pltpu.VMEM((n_plane, 8, LANES), f32),
        pltpu.VMEM((n_z, 8, LANES), f32),
        pltpu.VMEM((PIECES, 8, LANES), f32),
        pltpu.SemaphoreType.DMA((3,)),
        pltpu.SemaphoreType.DMA((8,)),
        pltpu.SemaphoreType.DMA((8,)),
        pltpu.SemaphoreType.DMA((3,)),
        pltpu.SemaphoreType.DMA((3,)),
    ]
    cells = rows * PACK * n_plane * n_z
    scale = float(1.0 / (cells**0.5))
    in_grad, filter_grad = pl.pallas_call(
        functools.partial(kernel, geometry, scale),
        out_shape=(
            jax.ShapeDtypeStruct(inputs.shape, bf16),
            jax.ShapeDtypeStruct(filters.shape, f32),
        ),
        in_specs=[pl.BlockSpec(memory_space=pltpu.HBM)] * 3,
        out_specs=[pl.BlockSpec(memory_space=pltpu.VMEM)] * 2,
        scratch_shapes=scratch,
        compiler_params=pltpu.CompilerParams(
            collective_id=0, has_side_effects=True, vmem_limit_bytes=48 * 1024 * 1024
        ),
    )(*(pltpu.with_memory_space_constraint(value, pltpu.HBM) for value in (inputs, out_grad, filters)))
    in_grad, filter_grad = pl.pallas_call(
        put_out,
        out_shape=(
            jax.ShapeDtypeStruct(in_grad.shape, bf16),
            jax.ShapeDtypeStruct(filter_grad.shape, f32),
        ),
        in_specs=[pl.BlockSpec(memory_space=pltpu.VMEM)] * 2,
        out_specs=[pl.BlockSpec(memory_space=pltpu.HBM)] * 2,
        scratch_shapes=[pltpu.SemaphoreType.DMA((2,))],
        compiler_params=pltpu.CompilerParams(vmem_limit_bytes=8 * 1024 * 1024),
    )(in_grad, filter_grad)
    return in_grad, filter_grad.T


def solution(mesh):
    n_gz, n_ch = mesh.shape["gz"], mesh.shape["ch"]
    n_zlo, n_core, n_zhi = 4, 2, 3
    geometry = (n_gz // (n_zlo * n_core), n_zlo, n_core, n_zhi, n_ch // n_zhi)
    placed = (P("gz", "ch", None), P("gz", "ch", None), P())
    return jax.shard_map(
        functools.partial(per_device, geometry),
        mesh=mesh,
        in_specs=placed,
        out_specs=(P("gz", "ch", None), P()),
        check_vma=False,
    )
```

```python
import functools

import jax
import jax.numpy as jnp
from jax import lax
from jax.experimental import pallas as pl
from jax.experimental.pallas import tpu as pltpu
from jax.sharding import PartitionSpec as P

MESH = pl.DeviceIdType.MESH
CH = 32
LANES = 128
PACK = LANES // CH
PIECES = 64
TAPS = 27


def kernel(
    geometry,
    scale,
    x_hbm,
    og_hbm,
    f_hbm,
    in_grad,
    filter_grad,
    x_v,
    og_v,
    f_v,
    rows32,
    edge,
    z_low,
    z_high,
    y_side,
    y_side32,
    tail,
    bands,
    xt,
    windows,
    grads,
    pieces,
    parts,
    layers,
    whole,
    local_sem,
    halo_send,
    halo_recv,
    ring_send,
    ring_recv,
):
    n_x, n_zlo, n_core, n_zhi, n_y = geometry
    depth, height, width = x_hbm.shape
    groups = width // LANES
    group_rows = depth * height
    n_gz, n_ch = n_x * n_zlo * n_core, n_zhi * n_y
    n_plane, n_z = n_x * n_y * n_core, n_zhi * n_zlo

    gz, ch = lax.axis_index("gz"), lax.axis_index("ch")
    core = lax.rem(gz, n_core)
    z_lo = lax.rem(gz // n_core, n_zlo)
    x = gz // (n_core * n_zlo)
    z_hi, y = ch // n_y, lax.rem(ch, n_y)
    rank = (x * n_y + y) * n_core + core
    z = z_hi * n_zlo + z_lo

    def ways(size):
        return sorted(range(size), key=lambda move: -min(move, size - move))

    def moved(place, move, size):
        return place if move == 0 else lax.rem(place + move, size)

    x_at = [moved(x, move, n_x) for move in range(n_x)]
    core_at = [moved(core, move, n_core) for move in range(n_core)]
    near_moves = [(mx, mc) for mx in ways(n_x) for mc in ways(n_core)]

    def plane_walk(act):
        def row(my, there, alone):
            for mx, mc in near_moves:
                if alone and mx == 0 and mc == 0:
                    continue
                gz_there = (x_at[mx] * n_zlo + z_lo) * n_core + core_at[mc]
                rank_there = (x_at[mx] * n_y + there) * n_core + core_at[mc]
                act((gz_there, z_hi * n_y + there), rank_there, my * (n_x * n_core) + mx * n_core + mc - 1)

        half = n_y // 2
        row(half, lax.rem(y + half, n_y), False)

        @pl.loop(1, half)
        def _(j):
            row(half + j, lax.rem(y + half + j, n_y), False)
            row(half - j, lax.rem(y + half - j, n_y), False)

        row(0, y, True)

    z_moves = [(mh, ml) for mh in ways(n_zhi) for ml in ways(n_zlo) if mh or ml]
    z_peers = [
        ((x * n_zlo + moved(z_lo, ml, n_zlo)) * n_core + core, moved(z_hi, mh, n_zhi) * n_y + y) for mh, ml in z_moves
    ]

    up, down = lax.rem(gz + 1, n_gz), lax.rem(gz + n_gz - 1, n_gz)
    right, left = lax.rem(ch + 1, n_ch), lax.rem(ch + n_ch - 1, n_ch)
    neighbours = [(up, ch), (down, ch), (gz, right), (gz, left), (up, right), (down, right), (up, left), (down, left)]

    loads = [
        pltpu.make_async_copy(og_hbm, og_v, local_sem.at[0]),
        pltpu.make_async_copy(x_hbm, x_v, local_sem.at[1]),
        pltpu.make_async_copy(f_hbm, f_v, local_sem.at[2]),
    ]
    for load in loads:
        load.start()

    barrier = pltpu.get_barrier_semaphore()
    for device in neighbours:
        pl.semaphore_signal(barrier, inc=1, device_id=device, device_id_type=MESH)

    def greet(device, *_):
        pl.semaphore_signal(barrier, inc=1, device_id=device, device_id_type=MESH)

    for device in z_peers:
        greet(device)
    plane_walk(greet)

    lane = lax.broadcasted_iota(jnp.int32, (height, LANES), 1) // CH
    row = lax.broadcasted_iota(jnp.int32, (height, LANES), 0)

    def tile(ref, layer, g):
        return ref[layer, :, g * LANES : (g + 1) * LANES].astype(jnp.float32)

    loads[0].wait()
    for layer in range(depth):
        for g in range(groups):
            block = tile(og_v, layer, g)
            rows32[layer, g : g + 1, :] = block[0:1]
            rows32[depth + layer, g : g + 1, :] = block[height - 1 : height]
    for k in range(2 * depth):
        edge[k] = rows32[k].astype(jnp.bfloat16)

    pl.semaphore_wait(barrier, len(neighbours) + (n_z - 1) + (n_plane - 1))

    halo = [
        (edge.at[pl.ds(depth, depth)], y_side.at[0, pl.ds(1, depth)]),
        (edge.at[pl.ds(0, depth)], y_side.at[1, pl.ds(1, depth)]),
        (edge.at[depth + depth - 1], y_side.at[0, 0]),
        (edge.at[depth], y_side.at[0, depth + 1]),
        (edge.at[depth - 1], y_side.at[1, 0]),
        (edge.at[0], y_side.at[1, depth + 1]),
    ]
    halo = [(og_v.at[depth - 1], z_low), (og_v.at[0], z_high)] + halo
    sends = [
        pltpu.make_async_remote_copy(
            src_ref=source,
            dst_ref=target,
            send_sem=halo_send.at[k],
            recv_sem=halo_recv.at[k],
            device_id=neighbours[k],
            device_id_type=MESH,
        )
        for k, (source, target) in enumerate(halo)
    ]
    for k in (4, 5, 6, 7, 2, 3, 0, 1):
        sends[k].start()
    loads[2].wait()
    wide = lax.broadcasted_iota(jnp.int32, (CH, LANES), 1) // CH
    last = f_v.shape[1] // LANES
    tiles = [f_v[:, k * LANES : (k + 1) * LANES].astype(jnp.float32) for k in range(last)]
    tail[:, : f_v.shape[1] - last * LANES] = f_v[:, last * LANES :].astype(jnp.float32)
    tiles.append(tail[...])
    for w in range(9):
        place, turn = (3 * w) // PACK, (3 * w) % PACK
        slab = tiles[place]
        if turn:
            joined = slab if turn == 1 else jnp.where(wide >= turn, slab, tiles[place + 1])
            slab = pltpu.roll(joined, LANES - CH * turn, 1)
        for c_from in range(PACK):
            start = w * LANES + c_from * CH
            turn = (c_from - 1) % PACK
            band = pltpu.roll(slab, CH * turn, 1) if turn else slab
            used = wide != (c_from + 2) % PACK
            inside = used
            outside = jnp.zeros_like(band)
            if c_from == 0:
                inside = wide < 2
                outside = jnp.where(wide == PACK - 1, band, 0.0)
            elif c_from == PACK - 1:
                inside = wide >= 2
                outside = jnp.where(wide == 0, band, 0.0)
            bands[start : start + CH, :LANES] = jnp.where(inside, band, 0.0).astype(jnp.bfloat16)
            bands[start : start + CH, LANES:] = outside.astype(jnp.bfloat16)

    loads[1].wait()
    blocks = [jnp.concatenate([tile(x_v, layer, g) for layer in range(depth)], axis=0) for g in range(groups)]
    tall = lax.broadcasted_iota(jnp.int32, (group_rows, LANES), 1) // CH
    step = 8
    for g0 in range(0, groups, step):
        own = jnp.concatenate(blocks[g0 : g0 + step], axis=0)
        outer = jnp.concatenate(
            [
                jnp.where(tall < PACK // 2, blocks[(g + 1) % groups], blocks[(g - 1) % groups])
                for g in range(g0, g0 + step)
            ],
            axis=0,
        )
        columns = slice(g0 * group_rows, (g0 + step) * group_rows)
        xt[0:LANES, columns] = own.T.astype(jnp.bfloat16)
        xt[LANES : 2 * LANES, columns] = outer.T.astype(jnp.bfloat16)

    for send in sends:
        send.wait_recv()

    for side in range(2):
        for layer in range(depth + 2):
            y_side32[side, layer] = y_side[side, layer].astype(jnp.float32)

    for g in range(groups):
        cut = slice(g * LANES, (g + 1) * LANES)
        planes = [z_low[:, cut].astype(jnp.float32)]
        planes += [tile(og_v, layer, g) for layer in range(depth)]
        planes += [z_high[:, cut].astype(jnp.float32)]
        turned = [[], planes, []]
        for layer, plane in enumerate(planes):
            low = jnp.broadcast_to(y_side32[0, layer, g : g + 1, :], plane.shape)
            high = jnp.broadcast_to(y_side32[1, layer, g : g + 1, :], plane.shape)
            turned[2].append(jnp.where(row == 0, low, pltpu.roll(plane, 1, 0)))
            turned[0].append(jnp.where(row == height - 1, high, pltpu.roll(plane, height - 1, 0)))
        for kz in range(3):
            for ky in range(3):
                w = 3 * kz + ky
                block = jnp.concatenate(turned[ky][2 - kz : 2 - kz + depth], axis=0)
                windows[g * group_rows : (g + 1) * group_rows, w * LANES : (w + 1) * LANES] = block.astype(
                    jnp.bfloat16
                )

    grads[...] = jnp.dot(xt[...], windows[...], preferred_element_type=jnp.float32)

    def blocks_of(tap, t):
        if tap >= TAPS:
            return jnp.zeros((8, LANES), jnp.float32)
        w, kx = tap // 3, tap % 3
        total = None
        for c_from in range(PACK):
            c = c_from + kx - 1
            block = c if 0 <= c < PACK else (PACK if c == PACK else 2 * PACK - 1)
            start = block * CH + t * 8
            value = grads[start : start + 8, w * LANES : (w + 1) * LANES]
            total = value if total is None else jnp.where(lane == c_from, value, total)
        return total

    near, even = lane < 2, lane % 2 == 0
    for half in range(2):
        for k in range(PACK):
            for t in range(PACK):
                sums = [blocks_of(PACK * (PACK * half + n) + k, t) for n in range(PACK)]
                first = jnp.where(near, sums[0], sums[2]) + pltpu.roll(jnp.where(near, sums[2], sums[0]), 64, 1)
                second = jnp.where(near, sums[1], sums[3]) + pltpu.roll(jnp.where(near, sums[3], sums[1]), 64, 1)
                other = jnp.where(even, second, first)
                packed = jnp.where(even, first, second) + jnp.where(
                    even, pltpu.roll(other, LANES - CH, 1), pltpu.roll(other, CH, 1)
                )
                place = 2 * ((half * PACK + k) * PACK + t)
                pieces[place] = packed[0:4]
                pieces[place + 1] = packed[4:8]

    def send_part(device, rank_there, offset):
        pltpu.make_async_remote_copy(
            src_ref=pieces.at[rank_there],
            dst_ref=parts.at[offset],
            send_sem=ring_send.at[0],
            recv_sem=ring_recv.at[0],
            device_id=device,
            device_id_type=MESH,
        ).start()

    plane_walk(send_part)

    wide_out = lax.dot_general(
        windows[...], bands[...], (((1,), (0,)), ((), ())), preferred_element_type=jnp.float32
    )
    own = wide_out[:, :LANES]
    outer = wide_out[:, LANES:]
    for g in range(groups):
        for layer in range(depth):

            def rows(value, group, layer=layer):
                start = (group % groups) * group_rows + layer * height
                return value[start : start + height]

            result = rows(own, g) + jnp.where(lane < PACK // 2, rows(outer, g - 1), rows(outer, g + 1))
            in_grad[layer, :, g * LANES : (g + 1) * LANES] = result.astype(jnp.bfloat16)

    def all_but_one(ref, sem):
        count = ref.shape[0] - 1
        return pltpu.make_async_copy(ref.at[pl.ds(0, count)], ref.at[pl.ds(0, count)], ring_recv.at[sem])

    pltpu.make_async_copy(parts, parts, ring_recv.at[0]).wait()
    total = pieces[rank]
    for k in range(n_plane - 1):
        total = total + parts[k]
    layers[z] = total

    for device in z_peers:
        pltpu.make_async_remote_copy(
            src_ref=layers.at[z],
            dst_ref=layers.at[z],
            send_sem=ring_send.at[1],
            recv_sem=ring_recv.at[1],
            device_id=device,
            device_id_type=MESH,
        ).start()

    all_but_one(layers, 1).wait()
    total = layers[0]
    for k in range(1, n_z):
        total = total + layers[k]
    whole[rank] = total * scale

    def send_whole(device, *_):
        pltpu.make_async_remote_copy(
            src_ref=whole.at[rank],
            dst_ref=whole.at[rank],
            send_sem=ring_send.at[2],
            recv_sem=ring_recv.at[2],
            device_id=device,
            device_id_type=MESH,
        ).start()

    plane_walk(send_whole)

    all_but_one(whole, 2).wait()
    for half in range(2):
        start = half * PIECES // 2
        block = jnp.concatenate([whole[start + k] for k in range(PIECES // 2)], axis=0).T
        for n in range(PACK):
            column = (half * PACK + n) * LANES
            count = min(LANES, f_v.shape[1] - column)
            if count > 0:
                filter_grad[:, column : column + count] = block[n * CH : (n + 1) * CH, :count]

    for send in sends:
        send.wait_send()
    pltpu.make_async_copy(parts, parts, ring_send.at[0]).wait()
    pltpu.make_async_copy(layers.at[pl.ds(0, n_z - 1)], layers.at[pl.ds(0, n_z - 1)], ring_send.at[1]).wait()
    pltpu.make_async_copy(parts, parts, ring_send.at[2]).wait()


def put_out(in_grad_v, filter_grad_v, in_grad, filter_grad, sems):
    copies = [
        pltpu.make_async_copy(filter_grad_v, filter_grad, sems.at[0]),
        pltpu.make_async_copy(in_grad_v, in_grad, sems.at[1]),
    ]
    for copy in copies:
        copy.start()
    for copy in copies:
        copy.wait()


def per_device(geometry, inputs, out_grad, filters):
    depth, height, width = inputs.shape
    filters = filters.T
    n_x, n_zlo, n_core, n_zhi, n_y = geometry
    n_plane, n_z = n_x * n_y * n_core, n_zhi * n_zlo
    groups = width // LANES
    rows = depth * height * groups
    bf16, f32 = jnp.bfloat16, jnp.float32
    scratch = [
        pltpu.VMEM((depth, height, width), bf16),
        pltpu.VMEM((depth, height, width), bf16),
        pltpu.VMEM(filters.shape, bf16),
        pltpu.VMEM((2 * depth, groups, LANES), f32),
        pltpu.VMEM((2 * depth, groups, LANES), bf16),
        pltpu.VMEM((height, width), bf16),
        pltpu.VMEM((height, width), bf16),
        pltpu.VMEM((2, depth + 2, groups, LANES), bf16),
        pltpu.VMEM((2, depth + 2, groups, LANES), f32),
        pltpu.VMEM((CH, LANES), f32),
        pltpu.VMEM((9 * LANES, 2 * LANES), bf16),
        pltpu.VMEM((2 * LANES, rows), bf16),
        pltpu.VMEM((rows, 9 * LANES), bf16),
        pltpu.VMEM((2 * LANES, 9 * LANES), f32),
        pltpu.VMEM((PIECES, 4, LANES), f32),
        pltpu.VMEM((n_plane - 1, 4, LANES), f32),
        pltpu.VMEM((n_z, 4, LANES), f32),
        pltpu.VMEM((n_plane, 4, LANES), f32),
        pltpu.SemaphoreType.DMA((3,)),
        pltpu.SemaphoreType.DMA((8,)),
        pltpu.SemaphoreType.DMA((8,)),
        pltpu.SemaphoreType.DMA((3,)),
        pltpu.SemaphoreType.DMA((3,)),
    ]
    cells = rows * PACK * n_plane * n_z
    scale = float(1.0 / (cells**0.5))
    in_grad, filter_grad = pl.pallas_call(
        functools.partial(kernel, geometry, scale),
        out_shape=(
            jax.ShapeDtypeStruct(inputs.shape, bf16),
            jax.ShapeDtypeStruct(filters.shape, f32),
        ),
        in_specs=[pl.BlockSpec(memory_space=pltpu.HBM)] * 3,
        out_specs=[pl.BlockSpec(memory_space=pltpu.VMEM)] * 2,
        scratch_shapes=scratch,
        compiler_params=pltpu.CompilerParams(
            collective_id=0, has_side_effects=True, vmem_limit_bytes=48 * 1024 * 1024
        ),
    )(*(pltpu.with_memory_space_constraint(value, pltpu.HBM) for value in (inputs, out_grad, filters)))
    in_grad, filter_grad = pl.pallas_call(
        put_out,
        out_shape=(
            jax.ShapeDtypeStruct(in_grad.shape, bf16),
            jax.ShapeDtypeStruct(filter_grad.shape, f32),
        ),
        in_specs=[pl.BlockSpec(memory_space=pltpu.VMEM)] * 2,
        out_specs=[pl.BlockSpec(memory_space=pltpu.HBM)] * 2,
        scratch_shapes=[pltpu.SemaphoreType.DMA((2,))],
        compiler_params=pltpu.CompilerParams(vmem_limit_bytes=8 * 1024 * 1024),
    )(in_grad, filter_grad)
    return in_grad, filter_grad.T


def solution(mesh):
    n_gz, n_ch = mesh.shape["gz"], mesh.shape["ch"]
    n_zlo, n_core, n_zhi = 4, 2, 3
    geometry = (n_gz // (n_zlo * n_core), n_zlo, n_core, n_zhi, n_ch // n_zhi)
    placed = (P("gz", "ch", None), P("gz", "ch", None), P())
    return jax.shard_map(
        functools.partial(per_device, geometry),
        mesh=mesh,
        in_specs=placed,
        out_specs=(P("gz", "ch", None), P()),
        check_vma=False,
    )
```
